32 devices in a mesh: band: 4 (over y, x), sector: 8 (over z, core).
Axes of the slice: x: 2, y: 2, z: 4, core: 2. Of those that a mesh axis runs over, the one named last changes fastest.
Arguments:
- grid_lat: bfloat16 [32, 512, 512], P('band', 'sector'), may hold values from -6 to 6
- mesh_lat: bfloat16 [4096, 512], P(('band', 'sector')), may hold values from -6 to 6
- edge_feat: bfloat16 [49152, 512], P(('band', 'sector')), may hold values from -6 to 6
- edge_src: int32 [49152], P(('band', 'sector')), may hold values from 0 to 255, as said below
- edge_dst: int32 [49152], P(('band', 'sector')), may hold values from 0 to 511, as said below
- send_rows: int32 [4096], P(('band', 'sector')), may hold values from 0 to 127
- w_edge1: bfloat16 [1536, 512], replicated, may hold values from -0.15625 to 0.15625
- w_edge2: bfloat16 [512, 512], replicated, may hold values from -0.25 to 0.25
- edge_gain: float32 [512], replicated, may hold values from 0.25 to 1.75
- w_node1: bfloat16 [1024, 512], replicated, may hold values from -0.1875 to 0.1875
- w_node2: bfloat16 [512, 512], replicated, may hold values from -0.25 to 0.25
- node_gain: float32 [512], replicated, may hold values from 0.25 to 1.75
- cotangent: bfloat16 [32, 512, 512], P('band', 'sector'), may hold values from -6 to 6
Outputs:
- grid_out: bfloat16 [32, 512, 512], P('band', 'sector')
- grad_grid: bfloat16 [32, 512, 512], P('band', 'sector')
- grad_mesh: bfloat16 [4096, 512], P(('band', 'sector'))
- grad_w_edge1: float32 [1536, 512], P('sector')
The draws below stay inside these ranges and needn't reach their ends.
Inputs may be any that keep to these rules, and one draw needn't show every extreme that they name: `edge_src`: A device's mesh table is its 128 own rows followed by 32 rows each from the sector neighbour below, the sector neighbour above, the band neighbour below and the band neighbour above; devices of the first band never read the rows from below, those of the last band never the rows from above. `edge_dst`: each grid point of a device is the destination of exactly 3 of that device's edges; edges are in no particular order.
All inputs are finite; a program needn't handle non-finite values.
Results may differ from the reference program's by a relative error of at most 0.02.
Values may be sent and summed in bfloat16 or wider, within the bound.
A program may use at most 64 MiB of HBM per device.

```python
import math
import jax
import jax.numpy as jnp
from jax import lax

D = 512
LAT_DEV = 8
LON_DEV = 64
MESH_DEV = 128
HALO = 32
GRID_DEV = 512
EDGE_DEV = 1536
TABLE = 256
BANDS = 4
SECTORS = 8
LAT = 32
LON = 512
EDGES = 49152
MESH = 4096
SENDS = 4096
N_BAND = 4
N_SECTOR = 8
DEVICES = 32


def draw_edge_src(key, part):
    picked_rows = jax.random.randint(key, (DEVICES, EDGE_DEV), 0, MESH_DEV + 4 * HALO)
    band_index = (jnp.arange(DEVICES) // SECTORS)[:, None]
    below_start = MESH_DEV + 2 * HALO
    above_start = MESH_DEV + 3 * HALO
    first_band = (band_index == 0) & (picked_rows >= below_start) & (picked_rows < above_start)
    last_band = (band_index == BANDS - 1) & (picked_rows >= above_start)
    picked_rows = jnp.where(first_band, picked_rows - below_start, picked_rows)
    picked_rows = jnp.where(last_band, picked_rows - above_start, picked_rows)
    return picked_rows.reshape(-1).astype(jnp.int32)


def shuffled_order(subkey):
    return jax.random.permutation(subkey, EDGE_DEV)


def draw_edge_dst(key, part):
    subkeys = jax.random.split(key, DEVICES)
    orders = jax.vmap(shuffled_order)(subkeys)
    return (orders // 3).reshape(-1).astype(jnp.int32)


def place_ends(drawn, key, least, largest):
    spot = [jax.random.randint(jax.random.fold_in(key, axis), (), 0, length) for axis, length in enumerate(drawn.shape)]
    main_axis = drawn.shape.index(max(drawn.shape))
    neighbour = spot[:main_axis] + [(spot[main_axis] + 1) % drawn.shape[main_axis]] + spot[main_axis + 1:]
    return drawn.at[tuple(spot)].set(least).at[tuple(neighbour)].set(largest)


def strengthened(array, rng, source, target, parts, factor):
    owner, partner = [(jnp.arange(array.shape[position]) // (array.shape[position] // parts)).reshape([-1 if axis == position else 1 for axis in range(array.ndim)]) for position in (source, target)]
    chosen = jax.random.permutation(rng, parts)[partner]
    strong = (owner == chosen) | (owner == (partner + parts // 2) % parts)
    return jnp.where(strong, factor * array, array)


def steps_of(own_key, extent, cuts, least, largest):
    loudness, own = 1.0, jax.random.fold_in(own_key, 6)
    for axis_at, shards_of in cuts:
        draws = jnp.exp(jax.random.uniform(jax.random.fold_in(own, axis_at), (shards_of,), jnp.float32, least / len(cuts), largest / len(cuts)))
        loudness = loudness * jnp.repeat(draws, extent[axis_at] // shards_of).reshape([-1 if axis == axis_at else 1 for axis in range(len(extent))])
    return loudness


def normal_values(own_key, dims, deviation, bound, pieces=(), held_as=jnp.bfloat16):
    level = steps_of(own_key, dims, pieces, -0.22, 0.18) if pieces else 1.0
    array = jax.random.normal(own_key, dims, jnp.float32) * deviation * level
    return jnp.minimum(jnp.maximum(array, -bound), bound).astype(held_as)


def noise_with(key, shape, width, reach, cuts, heavy, kind=jnp.bfloat16):
    drawn = width * jax.random.normal(key, shape, jnp.float32)
    if cuts:
        drawn = drawn * steps_of(key, shape, cuts, -0.22, 0.18)
    return jnp.clip(strengthened(drawn, jax.random.fold_in(key, 3), *heavy), -reach, reach).astype(kind)


def setup_inputs(seed: int = 0) -> dict:
    key_of = jax.random.split(jax.random.key(seed), 14)
    return {
        "grid_lat": normal_values(key_of[0], (LAT, LON, D), 1.0, 6.0, ((0, 4), (1, 8))),
        "mesh_lat": normal_values(key_of[1], (MESH, D), 1.0, 6.0, ((0, 32),)),
        "edge_feat": noise_with(key_of[2], (EDGES, D), 1.0, 6.0, ((0, 32),), (0, 1, 32, 2.75)),
        "edge_src": draw_edge_src(jax.random.fold_in(key_of[13], 71), 0),
        "edge_dst": draw_edge_dst(jax.random.fold_in(key_of[13], 71), 0),
        "send_rows": place_ends(jax.random.randint(key_of[5], (SENDS,), 0, MESH_DEV), jax.random.fold_in(key_of[5], 1), 0, MESH_DEV - 1).astype(jnp.int32),
        "w_edge1": normal_values(key_of[6], (3 * D, D), (3 * D) ** -0.5, 0.15625),
        "w_edge2": normal_values(key_of[7], (D, D), D ** -0.5, 0.25),
        "edge_gain": jnp.clip(1.0 + 0.15 * jax.random.normal(key_of[8], (D,), jnp.float32), 0.25, 1.75),
        "w_node1": normal_values(key_of[9], (2 * D, D), (2 * D) ** -0.5, 0.1875),
        "w_node2": normal_values(key_of[10], (D, D), D ** -0.5, 0.25),
        "node_gain": jnp.clip(1.0 + 0.15 * jax.random.normal(key_of[11], (D,), jnp.float32), 0.25, 1.75),
        "cotangent": normal_values(key_of[12], (LAT, LON, D), 1.0, 6.0, ((0, 4), (1, 8))),
    }


EPSILON = 1e-05

def swish(values):
    return values * jax.nn.sigmoid(values)

def layer_norm(values, gain_vector):
    average = lax.optimization_barrier(jnp.mean(values, axis=-1, keepdims=True))
    centred = values - average
    spread = lax.optimization_barrier(jnp.mean(centred * centred, axis=-1, keepdims=True))
    return centred * lax.rsqrt(spread + EPSILON) * gain_vector

def decode_tail(pre_act, grid_wide, edge_dst, w_edge2, edge_gain, w_node1, w_node2, node_gain):
    hidden = swish(pre_act).astype(jnp.bfloat16)
    edge_raw = jnp.dot(hidden, w_edge2, preferred_element_type=jnp.float32)
    message = layer_norm(edge_raw, edge_gain).astype(jnp.bfloat16)
    points = grid_wide.shape[0]
    onehot = (edge_dst[None, :] == jnp.arange(points, dtype=jnp.int32)[:, None]).astype(jnp.bfloat16)
    aggregated = jnp.dot(onehot, message, preferred_element_type=jnp.float32).astype(jnp.bfloat16)
    node_input = jnp.concatenate([aggregated, grid_wide.astype(jnp.bfloat16)], axis=1)
    node_hidden = swish(jnp.dot(node_input, w_node1, preferred_element_type=jnp.float32)).astype(jnp.bfloat16)
    node_raw = jnp.dot(node_hidden, w_node2, preferred_element_type=jnp.float32)
    return (grid_wide + layer_norm(node_raw, node_gain)).astype(jnp.bfloat16)

def block_pass(mesh_table, grid_block, edge_block, edge_src, edge_dst, cot_block, w_edge1, w_edge2, edge_gain, w_node1, w_node2, node_gain):
    feature_width = w_edge2.shape[0]
    inputs = jnp.concatenate([edge_block, mesh_table[edge_src], grid_block[edge_dst]], axis=1)
    pre_act = jnp.dot(inputs, w_edge1, preferred_element_type=jnp.float32)
    grid_wide = grid_block.astype(jnp.float32)

    def finish(pre_values, grid_values):
        return decode_tail(pre_values, grid_values, edge_dst, w_edge2, edge_gain, w_node1, w_node2, node_gain)
    result, pullback = jax.vjp(finish, pre_act, grid_wide)
    grad_pre, grad_tail = pullback(cot_block)
    grad_pre_b = grad_pre.astype(jnp.bfloat16)
    grad_weight = lax.dot_general(inputs, grad_pre_b, (((0,), (0,)), ((), ())), preferred_element_type=jnp.float32)
    grad_inputs = lax.dot_general(grad_pre_b, w_edge1[feature_width:], (((1,), (1,)), ((), ())), preferred_element_type=jnp.float32)
    grad_table = jax.ops.segment_sum(grad_inputs[:, :feature_width], edge_src, num_segments=mesh_table.shape[0])
    grad_grid = grad_tail + jax.ops.segment_sum(grad_inputs[:, feature_width:], edge_dst, num_segments=grid_block.shape[0])
    return (result, grad_table, grad_grid, grad_weight)

def reference(grid_lat, mesh_lat, edge_feat, edge_src, edge_dst, send_rows, w_edge1, w_edge2, edge_gain, w_node1, w_node2, node_gain, cotangent):
    band_count = N_BAND
    sector_count = N_SECTOR
    blocks = band_count * sector_count
    feature_width = D
    mesh_blocks = mesh_lat.reshape(band_count, sector_count, MESH_DEV, feature_width)
    send_table = send_rows.reshape(band_count, sector_count, 4, HALO)

    def take_rows(rows_block, index_block):
        return rows_block[index_block]

    def select_part(part_index):
        return jax.vmap(jax.vmap(take_rows))(mesh_blocks, send_table[:, :, part_index, :])
    to_left = select_part(0)
    to_right = select_part(1)
    to_below = select_part(2)
    to_above = select_part(3)
    from_left = jnp.roll(to_right, 1, axis=1)
    from_right = jnp.roll(to_left, -1, axis=1)
    zero_rows = jnp.zeros_like(to_above[:1])
    from_below = jnp.concatenate([zero_rows, to_above[:-1]], axis=0)
    from_above = jnp.concatenate([to_below[1:], zero_rows], axis=0)
    tables = jnp.concatenate([mesh_blocks, from_left, from_right, from_below, from_above], axis=2)
    tables = tables.reshape(blocks, TABLE, feature_width)

    def to_blocks(field):
        shaped = field.reshape(band_count, LAT_DEV, sector_count, LON_DEV, feature_width)
        return shaped.transpose(0, 2, 1, 3, 4).reshape(blocks, GRID_DEV, feature_width)

    def from_blocks(field):
        shaped = field.reshape(band_count, sector_count, LAT_DEV, LON_DEV, feature_width)
        return shaped.transpose(0, 2, 1, 3, 4).reshape(LAT, LON, feature_width)
    grid_blocks = to_blocks(grid_lat)
    cot_blocks = to_blocks(cotangent)
    edge_blocks = edge_feat.reshape(blocks, EDGE_DEV, feature_width)
    src_blocks = edge_src.reshape(blocks, EDGE_DEV)
    dst_blocks = edge_dst.reshape(blocks, EDGE_DEV)

    def visit_block(running, block_items):
        mesh_table, grid_block, edge_block, src_block, dst_block, cot_block = block_items
        result, grad_table, grad_grid, grad_weight = block_pass(mesh_table, grid_block, edge_block, src_block, dst_block, cot_block, w_edge1, w_edge2, edge_gain, w_node1, w_node2, node_gain)
        return (running + grad_weight, (result, grad_table, grad_grid))
    start_sum = jnp.zeros((3 * feature_width, feature_width), jnp.float32)
    grad_weight, outputs = lax.scan(visit_block, start_sum, (tables, grid_blocks, edge_blocks, src_blocks, dst_blocks, cot_blocks))
    results, grad_tables, grad_grids = outputs
    grad_tables = grad_tables.reshape(band_count, sector_count, TABLE, feature_width)
    own_part = grad_tables[:, :, :MESH_DEV]
    grad_left = grad_tables[:, :, MESH_DEV:MESH_DEV + HALO]
    grad_right = grad_tables[:, :, MESH_DEV + HALO:MESH_DEV + 2 * HALO]
    grad_below = grad_tables[:, :, MESH_DEV + 2 * HALO:MESH_DEV + 3 * HALO]
    grad_above = grad_tables[:, :, MESH_DEV + 3 * HALO:]
    zero_grads = jnp.zeros_like(grad_above[:1])
    left_back = jnp.roll(grad_right, 1, axis=1)
    right_back = jnp.roll(grad_left, -1, axis=1)
    below_back = jnp.concatenate([zero_grads, grad_above[:-1]], axis=0)
    above_back = jnp.concatenate([grad_below[1:], zero_grads], axis=0)
    returned = jnp.concatenate([left_back, right_back, below_back, above_back], axis=2)
    send_index = send_rows.reshape(band_count, sector_count, 4 * HALO)

    def add_rows(values, index_block):
        return jax.ops.segment_sum(values, index_block, num_segments=MESH_DEV)
    scattered = jax.vmap(jax.vmap(add_rows))(returned, send_index)
    grad_mesh = (own_part + scattered).reshape(MESH, feature_width).astype(jnp.bfloat16)
    grid_out = from_blocks(results)
    grad_grid = from_blocks(grad_grids).astype(jnp.bfloat16)
    grad_w_edge1 = grad_weight * (1.0 / math.sqrt(EDGES))
    return (grid_out, grad_grid, grad_mesh, grad_w_edge1)
```

```python
import functools
import math

import jax
import jax.numpy as jnp
from jax import lax
from jax.experimental import pallas as pl
from jax.experimental.pallas import tpu as pltpu
from jax.sharding import PartitionSpec as P

EPSILON = 1e-05
MESH_ID = pl.DeviceIdType.MESH
F32 = jnp.float32
BF16 = jnp.bfloat16
VMEM_SPEC = pl.BlockSpec(memory_space=pltpu.VMEM)


def dot(a, b):
    return jnp.dot(a, b, preferred_element_type=F32)


def dot_t(a, b):
    return lax.dot_general(a, b, (((1,), (1,)), ((), ())), preferred_element_type=F32)


def t_dot(a, b):
    return lax.dot_general(a, b, (((0,), (0,)), ((), ())), preferred_element_type=F32)


def onehot_rows(index_row, count):
    width = index_row.shape[1]
    return (lax.broadcasted_iota(jnp.int32, (count, width), 0) == index_row).astype(F32).astype(BF16)


def neighbours():
    sectors, bands = lax.axis_size("sector"), lax.axis_size("band")
    s, b = lax.axis_index("sector"), lax.axis_index("band")
    below = {"sector": lax.rem(s + sectors - 1, sectors)}
    above = {"sector": lax.rem(s + 1, sectors)}
    band_below = {"band": lax.rem(b + bands - 1, bands)}
    band_above = {"band": lax.rem(b + 1, bands)}
    return below, above, band_below, band_above


def halo_kernel(mesh_ref, send_ref, out_ref, picked, landed, send_sem, recv_sem):
    below, above, band_below, band_above = neighbours()
    barrier = pltpu.get_barrier_semaphore()
    for other in (below, above, band_below, band_above):
        pl.semaphore_signal(barrier, inc=1, device_id=other, device_id_type=MESH_ID)
    margin = out_ref.shape[1]
    sel = onehot_rows(send_ref[...], mesh_ref.shape[0])
    rows = t_dot(sel, mesh_ref[...]).astype(BF16)
    for g in range(4):
        picked[g] = rows[g * margin : (g + 1) * margin]
    pl.semaphore_wait(barrier, 4)
    copies = []
    for g, (other, slot) in enumerate(((below, 1), (above, 0), (band_below, 3), (band_above, 2))):
        copy = pltpu.make_async_remote_copy(
            src_ref=picked.at[g],
            dst_ref=landed.at[slot],
            send_sem=send_sem.at[g],
            recv_sem=recv_sem.at[slot],
            device_id=other,
            device_id_type=MESH_ID,
        )
        copy.start()
        copies.append(copy)
    for copy in copies:
        copy.wait()
    out_ref[...] = landed[...]


def halo_exchange(mesh_lat, send_row):
    feature = mesh_lat.shape[1]
    margin = send_row.shape[1] // 4
    return pl.pallas_call(
        halo_kernel,
        out_shape=jax.ShapeDtypeStruct((4, margin, feature), BF16),
        in_specs=[VMEM_SPEC] * 2,
        out_specs=VMEM_SPEC,
        scratch_shapes=[
            pltpu.VMEM((4, margin, feature), BF16),
            pltpu.VMEM((4, margin, feature), BF16),
            pltpu.SemaphoreType.DMA((4,)),
            pltpu.SemaphoreType.DMA((4,)),
        ],
        compiler_params=pltpu.CompilerParams(collective_id=0, has_side_effects=True),
    )(mesh_lat, send_row)


def sigmoid(v):
    return jax.nn.sigmoid(v)


def compute_kernel(
    src_ref, dst_ref, grid_ref, own_ref, halo_ref, edge_ref, w1_ref, w2_ref, eg_ref,
    n1_ref, n2_ref, ng_ref, cot_ref,
    out_ref, gg_ref, gto_ref, gth_ref, dw_ref,
    table, proj, sel_t, sel, dsw, xhat, rstd, msg, dagg, tail, gp, red,
    *, edge_block, node_block,
):
    edges, width = edge_ref.shape
    points = grid_ref.shape[0]
    own = own_ref.shape[0]
    rows = own + halo_ref.shape[0]
    table[:own, :] = own_ref[...]
    table[own:, :] = halo_ref[...]
    proj[:rows, :] = dot(table[...], w1_ref[width : 2 * width, :]).astype(BF16)
    proj[rows:, :] = dot(grid_ref[...], w1_ref[2 * width :, :]).astype(BF16)

    def column_onehot(index_row, count):
        columns = jnp.broadcast_to(index_row, (128, index_row.shape[1])).T
        lanes = lax.broadcasted_iota(jnp.int32, columns.shape, 1)
        return [(columns == lanes + k).astype(F32).astype(BF16) for k in range(0, count, 128)]

    def forward(i, carry):
        at = pl.ds(pl.multiple_of(i * edge_block, edge_block), edge_block)
        src, dst = src_ref[:, at], dst_ref[:, at]
        sel_t[:rows, at] = onehot_rows(src, rows)
        sel_t[rows:, at] = onehot_rows(dst, points)
        both = jnp.concatenate(column_onehot(src, rows) + column_onehot(dst, points), axis=1)
        sel[at, :] = both
        pre = dot(edge_ref[at, :], w1_ref[:width, :]) + dot(both, proj[...])
        sig = sigmoid(pre)
        dsw[at, :] = sig * (1.0 + pre * (1.0 - sig))
        raw = dot((pre * sig).astype(BF16), w2_ref[...])
        centred = raw - jnp.mean(raw, axis=-1, keepdims=True)
        scale = lax.rsqrt(jnp.mean(centred * centred, axis=-1, keepdims=True) + EPSILON)
        normed = centred * scale
        xhat[at, :] = normed
        rstd[at, :] = jnp.broadcast_to(scale, (edge_block, 128))
        msg[at, :] = (normed * eg_ref[...]).astype(BF16)
        return carry

    lax.fori_loop(0, edges // edge_block, forward, 0)

    def nodes(i, carry):
        start = pl.multiple_of(i * node_block, node_block)
        at = pl.ds(start, node_block)
        agg = dot(sel_t[pl.ds(rows + start, node_block), :], msg[...]).astype(BF16)
        grid = grid_ref[at, :]
        pre = dot(agg, n1_ref[:width, :]) + dot(grid, n1_ref[width:, :])
        sig = sigmoid(pre)
        raw = dot((pre * sig).astype(BF16), n2_ref[...])
        centred = raw - jnp.mean(raw, axis=-1, keepdims=True)
        scale = lax.rsqrt(jnp.mean(centred * centred, axis=-1, keepdims=True) + EPSILON)
        normed = centred * scale
        out_ref[at, :] = (grid.astype(F32) + normed * ng_ref[...]).astype(BF16)
        cot = cot_ref[at, :].astype(F32)
        dnorm = cot * ng_ref[...]
        draw = scale * (
            dnorm
            - jnp.mean(dnorm, axis=-1, keepdims=True)
            - normed * jnp.mean(dnorm * normed, axis=-1, keepdims=True)
        )
        dhid = dot_t(draw.astype(BF16), n2_ref[...]).astype(BF16).astype(F32)
        dpre = (dhid * (sig * (1.0 + pre * (1.0 - sig)))).astype(BF16)
        dagg[at, :] = dot_t(dpre, n1_ref[:width, :]).astype(BF16)
        tail[at, :] = cot + dot_t(dpre, n1_ref[width:, :]).astype(BF16).astype(F32)
        return carry

    lax.fori_loop(0, points // node_block, nodes, 0)

    def backward(i, carry):
        at = pl.ds(pl.multiple_of(i * edge_block, edge_block), edge_block)
        dnorm = dot(sel[at, rows:], dagg[...]) * eg_ref[...]
        normed = xhat[at, :]
        draw = rstd[at, :1] * (
            dnorm
            - jnp.mean(dnorm, axis=-1, keepdims=True)
            - normed * jnp.mean(dnorm * normed, axis=-1, keepdims=True)
        )
        dhid = dot_t(draw.astype(BF16), w2_ref[...]).astype(BF16).astype(F32)
        gp[at, :] = (dhid * dsw[at, :]).astype(BF16)
        return carry

    lax.fori_loop(0, edges // edge_block, backward, 0)

    grads = gp[...]
    red[...] = dot(sel_t[...], grads).astype(BF16)
    dw_ref[:width, :] = t_dot(edge_ref[...], grads).astype(BF16)
    red_table, red_grid = red[:rows, :], red[rows:, :]
    dw_ref[width : 2 * width, :] = t_dot(table[...], red_table).astype(BF16)
    dw_ref[2 * width :, :] = t_dot(grid_ref[...], red_grid).astype(BF16)
    grad_table = dot_t(red_table, w1_ref[width : 2 * width, :])
    gto_ref[...] = grad_table[:own]
    gth_ref[...] = grad_table[own:].astype(BF16)
    gg_ref[...] = (tail[...] + dot_t(red_grid, w1_ref[2 * width :, :])).astype(BF16)


def local_compute(src, dst, grid, own, halo, edge, w1, w2, eg, n1, n2, ng, cot):
    edges, width = edge.shape
    points = grid.shape[0]
    rows = own.shape[0] + halo.shape[0]
    edge_block = math.gcd(edges, 256)
    node_block = math.gcd(points, 256)
    return pl.pallas_call(
        functools.partial(compute_kernel, edge_block=edge_block, node_block=node_block),
        out_shape=(
            jax.ShapeDtypeStruct((points, width), BF16),
            jax.ShapeDtypeStruct((points, width), BF16),
            jax.ShapeDtypeStruct(own.shape, F32),
            jax.ShapeDtypeStruct(halo.shape, BF16),
            jax.ShapeDtypeStruct(w1.shape, BF16),
        ),
        in_specs=[VMEM_SPEC] * 13,
        out_specs=(VMEM_SPEC,) * 5,
        scratch_shapes=[
            pltpu.VMEM((rows, width), BF16),
            pltpu.VMEM((rows + points, width), BF16),
            pltpu.VMEM((rows + points, edges), BF16),
            pltpu.VMEM((edges, rows + points), BF16),
            pltpu.VMEM((edges, width), F32),
            pltpu.VMEM((edges, width), F32),
            pltpu.VMEM((edges, 128), F32),
            pltpu.VMEM((edges, width), BF16),
            pltpu.VMEM((points, width), BF16),
            pltpu.VMEM((points, width), F32),
            pltpu.VMEM((edges, width), BF16),
            pltpu.VMEM((rows + points, width), BF16),
        ],
        compiler_params=pltpu.CompilerParams(vmem_limit_bytes=60 * 1024 * 1024),
    )(src, dst, grid, own, halo, edge, w1, w2, eg, n1, n2, ng, cot)


def reduce_kernel(
    dw_ref, gth_ref, gto_ref, send_ref, gw_ref, gm_ref,
    r0, a0, r1, a1, r2, fin, r3, ret,
    s0, v0, s1, v1, s2, v2, s3, v3, sh, vh,
    *, grad_scale,
):
    chunks, chips, bands, share, wide = r0.shape
    sectors = 2 * chips
    s, b = lax.axis_index("sector"), lax.axis_index("band")
    core, chip = lax.rem(s, 2), lax.div(s, 2)
    partner = {"sector": s + 1 - 2 * core}
    other_side = {"sector": lax.rem(s + 2 * core - 1 + sectors, sectors)}
    below, above, band_below, band_above = neighbours()
    band_at = [lax.rem(b + o, bands) for o in range(bands)]
    chip_at = [lax.rem(chip + o, chips) for o in range(chips)]
    band_dev = [{"band": band_at[o]} for o in range(1, bands)]
    chip_dev = [{"sector": 2 * chip_at[o] + core} for o in range(1, chips)]

    barrier = pltpu.get_barrier_semaphore()
    peers = [partner, other_side] + band_dev + chip_dev
    for other in peers:
        pl.semaphore_signal(barrier, inc=1, device_id=other, device_id_type=MESH_ID)
    pl.semaphore_wait(barrier, len(peers))

    pending = []

    def send(src, dst, send_sem, recv_sem, other):
        copy = pltpu.make_async_remote_copy(
            src_ref=src, dst_ref=dst, send_sem=send_sem, recv_sem=recv_sem,
            device_id=other, device_id_type=MESH_ID,
        )
        copy.start()
        pending.append(copy)
        return copy

    def cols(c):
        return pl.ds(c * wide, wide)

    first = [
        send(dw_ref.at[:, 1 - core, :, :, cols(c)], r0.at[c], s0.at[c], v0.at[c], partner)
        for c in range(chunks)
    ]
    halos = [
        send(gth_ref.at[g], ret.at[slot], sh.at[g], vh.at[slot], other)
        for g, (other, slot) in enumerate(
            ((below, 1), (above, 0), (band_below, 3), (band_above, 2))
        )
    ]
    second = []
    for c in range(chunks):
        first[c].wait_recv()
        for o in list(range(1, bands)) + [0]:
            at = band_at[o]
            mine = dw_ref[:, core, at, :, c * wide : (c + 1) * wide].astype(F32)
            a0[c, at] = (mine + r0[c, :, at].astype(F32)).astype(BF16)
            if o:
                second.append(
                    send(a0.at[c, at], r1.at[c, o - 1], s1.at[c, o - 1], v1.at[c, o - 1], band_dev[o - 1])
                )
    for copy in halos:
        copy.wait_recv()
    own = gm_ref.shape[0]
    returned = ret[...].reshape(4 * ret.shape[1], ret.shape[2])
    gm_ref[...] = (gto_ref[...] + dot(onehot_rows(send_ref[...], own), returned)).astype(BF16)

    third = []
    for c in range(chunks):
        total = a0[c, b].astype(F32)
        for o in range(1, bands):
            second[c * (bands - 1) + o - 1].wait_recv()
            total = total + r1[c, o - 1].astype(F32)
        a1[c] = total.astype(BF16)
        for o in range(1, chips):
            third.append(
                send(a1.at[c, chip_at[o]], r2.at[c, o - 1], s2.at[c, o - 1], v2.at[c, o - 1], chip_dev[o - 1])
            )
    last = []
    for c in range(chunks):
        total = a1[c, chip].astype(F32)
        for o in range(1, chips):
            third[c * (chips - 1) + o - 1].wait_recv()
            total = total + r2[c, o - 1].astype(F32)
        fin[c] = total.astype(BF16)
        for o in range(1, bands):
            last.append(
                send(fin.at[c], r3.at[c, o - 1], s3.at[c, o - 1], v3.at[c, o - 1], band_dev[o - 1])
            )
        gw_ref[b, :, c * wide : (c + 1) * wide] = fin[c].astype(F32) * grad_scale
    for c in range(chunks):
        for o in range(1, bands):
            last[c * (bands - 1) + o - 1].wait_recv()
            origin = lax.rem(b + bands - o, bands)
            gw_ref[origin, :, c * wide : (c + 1) * wide] = r3[c, o - 1].astype(F32) * grad_scale
    for copy in pending:
        copy.wait_send()


def reduce_gradients(dw, gth, gto, send_row, grad_scale):
    chips, _, bands, share, width = dw.shape
    margin = gth.shape[1]
    chunks = width // math.gcd(width, 256)
    wide = width // chunks
    dma = pltpu.SemaphoreType.DMA
    return pl.pallas_call(
        functools.partial(reduce_kernel, grad_scale=grad_scale),
        out_shape=(
            jax.ShapeDtypeStruct((bands, share, width), F32),
            jax.ShapeDtypeStruct(gto.shape, BF16),
        ),
        in_specs=[VMEM_SPEC] * 4,
        out_specs=(VMEM_SPEC,) * 2,
        scratch_shapes=[
            pltpu.VMEM((chunks, chips, bands, share, wide), BF16),
            pltpu.VMEM((chunks, bands, chips, share, wide), BF16),
            pltpu.VMEM((chunks, bands - 1, chips, share, wide), BF16),
            pltpu.VMEM((chunks, chips, share, wide), BF16),
            pltpu.VMEM((chunks, chips - 1, share, wide), BF16),
            pltpu.VMEM((chunks, share, wide), BF16),
            pltpu.VMEM((chunks, bands - 1, share, wide), BF16),
            pltpu.VMEM((4, margin, width), BF16),
            dma((chunks,)), dma((chunks,)),
            dma((chunks, bands - 1)), dma((chunks, bands - 1)),
            dma((chunks, chips - 1)), dma((chunks, chips - 1)),
            dma((chunks, bands - 1)), dma((chunks, bands - 1)),
            dma((4,)), dma((4,)),
        ],
        compiler_params=pltpu.CompilerParams(
            collective_id=1, has_side_effects=True, vmem_limit_bytes=60 * 1024 * 1024
        ),
    )(dw, gth, gto, send_row)


def shards(
    grid_lat, mesh_lat, edge_feat, edge_src, edge_dst, send_rows,
    w_edge1, w_edge2, edge_gain, w_node1, w_node2, node_gain, cotangent,
):
    width = w_edge2.shape[0]
    lat_rows, lon_cols = grid_lat.shape[:2]
    points = lat_rows * lon_cols
    bands, sectors = lax.axis_size("band"), lax.axis_size("sector")
    margin = send_rows.shape[0] // 4
    send_row = send_rows.reshape(1, -1)
    halo = halo_exchange(mesh_lat, send_row)
    out, gg, gto, gth, dw = local_compute(
        edge_src.reshape(1, -1),
        edge_dst.reshape(1, -1),
        grid_lat.reshape(points, width),
        mesh_lat,
        halo.reshape(4 * margin, width),
        edge_feat,
        w_edge1,
        w_edge2,
        edge_gain.reshape(1, -1),
        w_node1,
        w_node2,
        node_gain.reshape(1, -1),
        cotangent.reshape(points, width),
    )
    total_edges = edge_feat.shape[0] * bands * sectors
    share = w_edge1.shape[0] // (bands * sectors)
    gw, gm = reduce_gradients(
        dw.reshape(sectors // 2, 2, bands, share, width),
        gth.reshape(4, margin, width),
        gto,
        send_row,
        1.0 / math.sqrt(total_edges),
    )
    return (
        out.reshape(lat_rows, lon_cols, width),
        gg.reshape(lat_rows, lon_cols, width),
        gm,
        gw.reshape(bands * share, width),
    )


def solution(mesh):
    in_specs = (
        P("band", "sector", None),
        P(("band", "sector"), None),
        P(("band", "sector"), None),
        P(("band", "sector")),
        P(("band", "sector")),
        P(("band", "sector")),
        P(),
        P(),
        P(),
        P(),
        P(),
        P(),
        P("band", "sector", None),
    )
    out_specs = (
        P("band", "sector", None),
        P("band", "sector", None),
        P(("band", "sector"), None),
        P("sector", None),
    )
    return jax.shard_map(shards, mesh=mesh, in_specs=in_specs, out_specs=out_specs, check_vma=False)
```

```python
import functools
import math

import jax
import jax.numpy as jnp
from jax import lax
from jax.experimental import pallas as pl
from jax.experimental.pallas import tpu as pltpu
from jax.sharding import PartitionSpec as P

EPSILON = 1e-05
MESH_ID = pl.DeviceIdType.MESH
F32 = jnp.float32
BF16 = jnp.bfloat16
VMEM_SPEC = pl.BlockSpec(memory_space=pltpu.VMEM)


def dot(a, b):
    return jnp.dot(a, b, preferred_element_type=F32)


def dot_t(a, b):
    return lax.dot_general(a, b, (((1,), (1,)), ((), ())), preferred_element_type=F32)


def t_dot(a, b):
    return lax.dot_general(a, b, (((0,), (0,)), ((), ())), preferred_element_type=F32)


def onehot_rows(index_row, count):
    width = index_row.shape[1]
    return (lax.broadcasted_iota(jnp.int32, (count, width), 0) == index_row).astype(F32).astype(BF16)


def neighbours():
    sectors, bands = lax.axis_size("sector"), lax.axis_size("band")
    s, b = lax.axis_index("sector"), lax.axis_index("band")
    below = {"sector": lax.rem(s + sectors - 1, sectors)}
    above = {"sector": lax.rem(s + 1, sectors)}
    band_below = {"band": lax.rem(b + bands - 1, bands)}
    band_above = {"band": lax.rem(b + 1, bands)}
    return below, above, band_below, band_above


def sigmoid(v):
    return jax.nn.sigmoid(v)


def layer_stats(raw):
    centred = raw - jnp.mean(raw, axis=-1, keepdims=True)
    scale = lax.rsqrt(jnp.mean(centred * centred, axis=-1, keepdims=True) + EPSILON)
    return centred * scale, scale


def layer_back(dnorm, normed, scale):
    return scale * (
        dnorm
        - jnp.mean(dnorm, axis=-1, keepdims=True)
        - normed * jnp.mean(dnorm * normed, axis=-1, keepdims=True)
    )


def column_onehot(index_row, count):
    columns = jnp.broadcast_to(index_row, (128, index_row.shape[1])).T
    lanes = lax.broadcasted_iota(jnp.int32, columns.shape, 1)
    return [(columns == lanes + k).astype(F32).astype(BF16) for k in range(0, count, 128)]


def step_kernel(
    src_ref, dst_ref, send_ref, own_ref, eg_ref, ng_ref,
    w1_hbm, grid_hbm, edge_hbm, w2_hbm, n1_hbm, n2_hbm, cot_hbm,
    out_ref, gg_ref, gm_ref, gw_ref,
    w1_ref, grid_ref, edge_ref, w2_ref, n1_ref, n2_ref, cot_ref, load_sem,
    picked, landed, hs, hv,
    table, proj, sel_t, sel, dsw, xhat, rstd, msg, dagg, tail, gp, red,
    dw, r0, a0, r1, a1, r2, fin, r3, gth, ret,
    s0, v0, s1, v1, s2, v2, s3, v3, sh, vh,
    *, edge_block, node_block,
):
    chunks, chips, bands, share, wide = r0.shape
    sectors = 2 * chips
    s, b = lax.axis_index("sector"), lax.axis_index("band")
    core, chip = lax.rem(s, 2), lax.div(s, 2)
    partner = {"sector": s + 1 - 2 * core}
    other_side = {"sector": lax.rem(s + 2 * core - 1 + sectors, sectors)}
    below, above, band_below, band_above = neighbours()
    band_at = [lax.rem(b + o, bands) for o in range(bands)]
    chip_at = [lax.rem(chip + o, chips) for o in range(chips)]
    band_dev = [{"band": band_at[o]} for o in range(1, bands)]
    chip_dev = [{"sector": 2 * chip_at[o] + core} for o in range(1, chips)]
    routes = ((below, 1), (above, 0), (band_below, 3), (band_above, 2))

    barrier = pltpu.get_barrier_semaphore()
    peers = [partner, other_side] + band_dev + chip_dev
    for other in peers:
        pl.semaphore_signal(barrier, inc=1, device_id=other, device_id_type=MESH_ID)

    loads = []
    pairs = (
        (w1_hbm, w1_ref), (grid_hbm, grid_ref), (edge_hbm, edge_ref), (w2_hbm, w2_ref),
        (n1_hbm, n1_ref), (n2_hbm, n2_ref), (cot_hbm, cot_ref),
    )
    for k, (far, near) in enumerate(pairs):
        load = pltpu.make_async_copy(far, near, load_sem.at[k])
        load.start()
        loads.append(load)

    pending = []

    def send(src, dst, send_sem, recv_sem, other):
        copy = pltpu.make_async_remote_copy(
            src_ref=src, dst_ref=dst, send_sem=send_sem, recv_sem=recv_sem,
            device_id=other, device_id_type=MESH_ID,
        )
        copy.start()
        pending.append(copy)
        return copy

    edges, width = edge_ref.shape
    points = grid_ref.shape[0]
    own = own_ref.shape[0]
    margin = picked.shape[1]
    rows = own + 4 * margin
    send_sel = onehot_rows(send_ref[...], own)
    chosen = t_dot(send_sel, own_ref[...]).astype(BF16)
    for g in range(4):
        picked[g] = chosen[g * margin : (g + 1) * margin]
    pl.semaphore_wait(barrier, len(peers))
    halos = [
        send(picked.at[g], landed.at[slot], hs.at[g], hv.at[slot], other)
        for g, (other, slot) in enumerate(routes)
    ]

    loads[0].wait()
    loads[1].wait()
    proj[rows:, :] = dot(grid_ref[...], w1_ref[2 * width :, :]).astype(BF16)
    loads[2].wait()

    def prepare(i, carry):
        at = pl.ds(pl.multiple_of(i * edge_block, edge_block), edge_block)
        src = src_ref[at].reshape(1, edge_block)
        dst = dst_ref[at].reshape(1, edge_block)
        sel_t[:rows, at] = onehot_rows(src, rows)
        sel_t[rows:, at] = onehot_rows(dst, points)
        sel[at, :rows] = jnp.concatenate(column_onehot(src, rows), axis=1)
        to_grid = jnp.concatenate(column_onehot(dst, points), axis=1)
        sel[at, rows:] = to_grid
        dsw[at, :] = dot(edge_ref[at, :], w1_ref[:width, :]) + dot(to_grid, proj[rows:, :])
        return carry

    lax.fori_loop(0, edges // edge_block, prepare, 0)

    for copy in halos:
        copy.wait_recv()
    table[:own, :] = own_ref[...]
    for g in range(4):
        table[own + g * margin : own + (g + 1) * margin, :] = landed[g]
    proj[:rows, :] = dot(table[...], w1_ref[width : 2 * width, :]).astype(BF16)
    loads[3].wait()

    def forward(i, carry):
        at = pl.ds(pl.multiple_of(i * edge_block, edge_block), edge_block)
        pre = dsw[at, :] + dot(sel[at, :rows], proj[:rows, :])
        sig = sigmoid(pre)
        dsw[at, :] = sig * (1.0 + pre * (1.0 - sig))
        normed, scale = layer_stats(dot((pre * sig).astype(BF16), w2_ref[...]))
        xhat[at, :] = normed
        rstd[at, :] = jnp.broadcast_to(scale, (edge_block, 128))
        msg[at, :] = (normed * eg_ref[...]).astype(BF16)
        return carry

    lax.fori_loop(0, edges // edge_block, forward, 0)
    for load in loads[4:]:
        load.wait()

    def nodes(i, carry):
        start = pl.multiple_of(i * node_block, node_block)
        at = pl.ds(start, node_block)
        agg = dot(sel_t[pl.ds(rows + start, node_block), :], msg[...]).astype(BF16)
        grid = grid_ref[at, :]
        pre = dot(agg, n1_ref[:width, :]) + dot(grid, n1_ref[width:, :])
        sig = sigmoid(pre)
        normed, scale = layer_stats(dot((pre * sig).astype(BF16), n2_ref[...]))
        out_ref[at, :] = (grid.astype(F32) + normed * ng_ref[...]).astype(BF16)
        cot = cot_ref[at, :].astype(F32)
        draw = layer_back(cot * ng_ref[...], normed, scale)
        dhid = dot_t(draw.astype(BF16), n2_ref[...]).astype(BF16).astype(F32)
        dpre = (dhid * (sig * (1.0 + pre * (1.0 - sig)))).astype(BF16)
        dagg[at, :] = dot_t(dpre, n1_ref[:width, :]).astype(BF16)
        tail[at, :] = cot + dot_t(dpre, n1_ref[width:, :]).astype(BF16).astype(F32)
        return carry

    lax.fori_loop(0, points // node_block, nodes, 0)

    def backward(i, carry):
        at = pl.ds(pl.multiple_of(i * edge_block, edge_block), edge_block)
        dnorm = dot(sel[at, rows:], dagg[...]) * eg_ref[...]
        draw = layer_back(dnorm, xhat[at, :], rstd[at, :1])
        dhid = dot_t(draw.astype(BF16), w2_ref[...]).astype(BF16).astype(F32)
        gp[at, :] = (dhid * dsw[at, :]).astype(BF16)
        return carry

    lax.fori_loop(0, edges // edge_block, backward, 0)

    def put(c, start, value):
        stop = start + value.shape[0]
        for k in range(start // share, -(-stop // share)):
            low, high = max(k * share, start), min((k + 1) * share, stop)
            at = (k // bands // 2, k // bands % 2, k % bands)
            piece = value[low - start : high - start].astype(BF16)
            dw[c, at[0], at[1], at[2], low - k * share : high - k * share] = piece

    first, second, third, last = [], [], [], []

    def band_stage(c):
        first[c].wait_recv()
        for o in list(range(1, bands)) + [0]:
            at = band_at[o]
            mine = dw[c, :, core, at].astype(F32)
            a0[c, at] = (mine + r0[c, :, at].astype(F32)).astype(BF16)
            if o:
                second.append(
                    send(a0.at[c, at], r1.at[c, o - 1], s1.at[c, o - 1], v1.at[c, o - 1], band_dev[o - 1])
                )

    for c in range(chunks):
        low, high = c * wide, (c + 1) * wide
        grads = gp[:, low:high]
        put(c, 0, t_dot(edge_ref[...], grads))
        part = dot(sel_t[...], grads).astype(BF16)
        red[:, low:high] = part
        put(c, width, t_dot(table[...], part[:rows]))
        put(c, 2 * width, t_dot(grid_ref[...], part[rows:]))
        first.append(send(dw.at[c, :, 1 - core], r0.at[c], s0.at[c], v0.at[c], partner))
        if c:
            band_stage(c - 1)
    grad_table = dot_t(red[:rows, :], w1_ref[width : 2 * width, :])
    for g in range(4):
        gth[g] = grad_table[own + g * margin : own + (g + 1) * margin].astype(BF16)
    backs = [
        send(gth.at[g], ret.at[slot], sh.at[g], vh.at[slot], other)
        for g, (other, slot) in enumerate(routes)
    ]
    band_stage(chunks - 1)
    gg_ref[...] = (tail[...] + dot_t(red[rows:, :], w1_ref[2 * width :, :])).astype(BF16)
    for copy in backs:
        copy.wait_recv()
    returned = ret[...].reshape(4 * margin, width)
    gm_ref[...] = (grad_table[:own] + dot(send_sel, returned)).astype(BF16)

    for c in range(chunks):
        total = a0[c, b].astype(F32)
        for o in range(1, bands):
            second[c * (bands - 1) + o - 1].wait_recv()
            total = total + r1[c, o - 1].astype(F32)
        a1[c] = total.astype(BF16)
        for o in range(1, chips):
            third.append(
                send(a1.at[c, chip_at[o]], r2.at[c, o - 1], s2.at[c, o - 1], v2.at[c, o - 1], chip_dev[o - 1])
            )
    for c in range(chunks):
        total = a1[c, chip].astype(F32)
        for o in range(1, chips):
            third[c * (chips - 1) + o - 1].wait_recv()
            total = total + r2[c, o - 1].astype(F32)
        fin[c] = total.astype(BF16)
        for o in range(1, bands):
            last.append(
                send(fin.at[c], r3.at[c, o - 1], s3.at[c, o - 1], v3.at[c, o - 1], band_dev[o - 1])
            )
        gw_ref[b, :, c * wide : (c + 1) * wide] = fin[c]
    for c in range(chunks):
        for o in range(1, bands):
            last[c * (bands - 1) + o - 1].wait_recv()
            origin = lax.rem(b + bands - o, bands)
            gw_ref[origin, :, c * wide : (c + 1) * wide] = r3[c, o - 1]
    for copy in pending:
        copy.wait_send()


def finish_kernel(grad_scale, out_in, gg_in, gm_in, gw_in, out_ref, gg_ref, gm_ref, gw_ref):
    out_ref[...] = out_in[...]
    gg_ref[...] = gg_in[...]
    gm_ref[...] = gm_in[...]
    gw_ref[...] = gw_in[...].astype(F32) * grad_scale


def decode_step(src, dst, send_row, own, eg, ng, w1, grid, edge, w2, n1, n2, cot):
    edges, width = edge.shape
    points = grid.shape[0]
    margin = send_row.shape[1] // 4
    rows = own.shape[0] + 4 * margin
    bands, sectors = lax.axis_size("band"), lax.axis_size("sector")
    chips = sectors // 2
    share = w1.shape[0] // (bands * sectors)
    chunks = width // math.gcd(width, 256)
    wide = width // chunks
    dma = pltpu.SemaphoreType.DMA
    whole = (w1, grid, edge, w2, n1, n2, cot)
    results = pl.pallas_call(
        functools.partial(
            step_kernel, edge_block=math.gcd(edges, 256), node_block=math.gcd(points, 256)
        ),
        out_shape=(
            jax.ShapeDtypeStruct((points, width), BF16),
            jax.ShapeDtypeStruct((points, width), BF16),
            jax.ShapeDtypeStruct(own.shape, BF16),
            jax.ShapeDtypeStruct((bands, share, width), BF16),
        ),
        in_specs=[VMEM_SPEC] * 6 + [pl.BlockSpec(memory_space=pl.ANY)] * 7,
        out_specs=(VMEM_SPEC,) * 4,
        scratch_shapes=[pltpu.VMEM(a.shape, a.dtype) for a in whole]
        + [
            dma((len(whole),)),
            pltpu.VMEM((4, margin, width), BF16),
            pltpu.VMEM((4, margin, width), BF16),
            dma((4,)), dma((4,)),
            pltpu.VMEM((rows, width), BF16),
            pltpu.VMEM((rows + points, width), BF16),
            pltpu.VMEM((rows + points, edges), BF16),
            pltpu.VMEM((edges, rows + points), BF16),
            pltpu.VMEM((edges, width), F32),
            pltpu.VMEM((edges, width), F32),
            pltpu.VMEM((edges, 128), F32),
            pltpu.VMEM((edges, width), BF16),
            pltpu.VMEM((points, width), BF16),
            pltpu.VMEM((points, width), F32),
            pltpu.VMEM((edges, width), BF16),
            pltpu.VMEM((rows + points, width), BF16),
            pltpu.VMEM((chunks, chips, 2, bands, share, wide), BF16),
            pltpu.VMEM((chunks, chips, bands, share, wide), BF16),
            pltpu.VMEM((chunks, bands, chips, share, wide), BF16),
            pltpu.VMEM((chunks, bands - 1, chips, share, wide), BF16),
            pltpu.VMEM((chunks, chips, share, wide), BF16),
            pltpu.VMEM((chunks, chips - 1, share, wide), BF16),
            pltpu.VMEM((chunks, share, wide), BF16),
            pltpu.VMEM((chunks, bands - 1, share, wide), BF16),
            pltpu.VMEM((4, margin, width), BF16),
            pltpu.VMEM((4, margin, width), BF16),
            dma((chunks,)), dma((chunks,)),
            dma((chunks, bands - 1)), dma((chunks, bands - 1)),
            dma((chunks, chips - 1)), dma((chunks, chips - 1)),
            dma((chunks, bands - 1)), dma((chunks, bands - 1)),
            dma((4,)), dma((4,)),
        ],
        compiler_params=pltpu.CompilerParams(
            collective_id=0, has_side_effects=True, vmem_limit_bytes=60 * 1024 * 1024
        ),
    )(src, dst, send_row, own, eg, ng, *whole)
    grad_scale = 1.0 / math.sqrt(edges * bands * sectors)
    return pl.pallas_call(
        functools.partial(finish_kernel, grad_scale),
        out_shape=tuple(
            jax.ShapeDtypeStruct(r.shape, F32 if k == 3 else BF16) for k, r in enumerate(results)
        ),
        in_specs=[VMEM_SPEC] * 4,
        out_specs=(VMEM_SPEC,) * 4,
    )(*results)


def shards(
    grid_lat, mesh_lat, edge_feat, edge_src, edge_dst, send_rows,
    w_edge1, w_edge2, edge_gain, w_node1, w_node2, node_gain, cotangent,
):
    width = w_edge2.shape[0]
    lat_rows, lon_cols = grid_lat.shape[:2]
    points = lat_rows * lon_cols
    out, gg, gm, gw = decode_step(
        edge_src,
        edge_dst,
        send_rows.reshape(1, -1),
        mesh_lat,
        edge_gain.reshape(1, -1),
        node_gain.reshape(1, -1),
        w_edge1,
        grid_lat.reshape(points, width),
        edge_feat,
        w_edge2,
        w_node1,
        w_node2,
        cotangent.reshape(points, width),
    )
    return (
        out.reshape(lat_rows, lon_cols, width),
        gg.reshape(lat_rows, lon_cols, width),
        gm,
        gw.reshape(-1, width),
    )


def solution(mesh):
    in_specs = (
        P("band", "sector", None),
        P(("band", "sector"), None),
        P(("band", "sector"), None),
        P(("band", "sector")),
        P(("band", "sector")),
        P(("band", "sector")),
        P(),
        P(),
        P(),
        P(),
        P(),
        P(),
        P("band", "sector", None),
    )
    out_specs = (
        P("band", "sector", None),
        P("band", "sector", None),
        P(("band", "sector"), None),
        P("sector", None),
    )
    return jax.shard_map(shards, mesh=mesh, in_specs=in_specs, out_specs=out_specs, check_vma=False)
```

```python
import functools
import math

import jax
import jax.numpy as jnp
from jax import lax
from jax.experimental import pallas as pl
from jax.experimental.pallas import tpu as pltpu
from jax.sharding import PartitionSpec as P

EPSILON = 1e-05
MESH_ID = pl.DeviceIdType.MESH
LANES = 128
GROUP = 2
F32 = jnp.float32
BF16 = jnp.bfloat16
VMEM_SPEC = pl.BlockSpec(memory_space=pltpu.VMEM)


def dot(a, b):
    return jnp.dot(a, b, preferred_element_type=F32)


def dot_t(a, b):
    return lax.dot_general(a, b, (((1,), (1,)), ((), ())), preferred_element_type=F32)


def t_dot(a, b):
    return lax.dot_general(a, b, (((0,), (0,)), ((), ())), preferred_element_type=F32)


def onehot_rows(index_row, count):
    width = index_row.shape[1]
    rows = lax.broadcasted_iota(jnp.int16, (count, width), 0)
    hit = rows == jnp.broadcast_to(index_row.astype(jnp.int16), (count, width))
    return jnp.where(hit, jnp.ones((), BF16), jnp.zeros((), BF16))


def neighbours():
    sectors, bands = lax.axis_size("sector"), lax.axis_size("band")
    s, b = lax.axis_index("sector"), lax.axis_index("band")
    below = {"sector": lax.rem(s + sectors - 1, sectors)}
    above = {"sector": lax.rem(s + 1, sectors)}
    band_below = {"band": lax.rem(b + bands - 1, bands)}
    band_above = {"band": lax.rem(b + 1, bands)}
    return below, above, band_below, band_above


def sigmoid(v):
    return 0.5 * jnp.tanh(0.5 * v) + 0.5


def layer_stats(raw):
    centred = raw - jnp.mean(raw, axis=-1, keepdims=True)
    scale = lax.rsqrt(jnp.mean(centred * centred, axis=-1, keepdims=True) + EPSILON)
    return centred * scale, scale


def layer_back(dnorm, normed, scale):
    return scale * (
        dnorm
        - jnp.mean(dnorm, axis=-1, keepdims=True)
        - normed * jnp.mean(dnorm * normed, axis=-1, keepdims=True)
    )


def column_onehot(index_row, count):
    columns = jnp.broadcast_to(index_row, (128, index_row.shape[1])).T
    columns = columns.astype(jnp.int16)
    lanes = lax.broadcasted_iota(jnp.int16, columns.shape, 1)
    one, zero = jnp.ones((), BF16), jnp.zeros((), BF16)
    return [
        jnp.where(columns - jnp.int16(k) == lanes, one, zero) for k in range(0, count, 128)
    ]


def step_kernel(
    src_ref, dst_ref, send_ref, own_ref, eg_ref, ng_ref,
    w1_hbm, grid_hbm, edge_hbm, w2_hbm, n1_hbm, n2_hbm, cot_hbm,
    out_ref, gg_ref, gm_ref, gw_ref,
    w1_ref, grid_ref, edge_ref, w2_ref, n1_ref, n2_ref, cot_ref, load_sem,
    picked, landed, hs, hv,
    table, proj, edge_t, grid_t, table_t, w2_t, sel_t, sel, dsw, xhat, rstd, msg, dagg, tail, gp, red,
    dw, r0, a0, r1, a1, r2, fin, r3, gth, ret,
    s0, v0, s1, v1, s2, v2, s3, v3, sh, vh,
    *, edge_block, node_block,
):
    chunks, chips, bands, share, wide = r0.shape
    sectors = 2 * chips
    s, b = lax.axis_index("sector"), lax.axis_index("band")
    core, chip = lax.rem(s, 2), lax.div(s, 2)
    partner = {"sector": s + 1 - 2 * core}
    other_side = {"sector": lax.rem(s + 2 * core - 1 + sectors, sectors)}
    below, above, band_below, band_above = neighbours()
    band_at = [lax.rem(b + o, bands) for o in range(bands)]
    chip_at = [lax.rem(chip + o, chips) for o in range(chips)]
    band_dev = [{"band": band_at[o]} for o in range(1, bands)]
    chip_dev = [{"sector": 2 * chip_at[o] + core} for o in range(1, chips)]
    routes = ((below, 1), (above, 0), (band_below, 3), (band_above, 2))

    barrier = pltpu.get_barrier_semaphore()
    peers = [partner, other_side] + band_dev + chip_dev
    for other in peers:
        pl.semaphore_signal(barrier, inc=1, device_id=other, device_id_type=MESH_ID)

    loads = []
    pairs = (
        (w1_hbm, w1_ref), (grid_hbm, grid_ref), (edge_hbm, edge_ref), (w2_hbm, w2_ref),
        (n1_hbm, n1_ref), (n2_hbm, n2_ref), (cot_hbm, cot_ref),
    )
    for k, (far, near) in enumerate(pairs):
        load = pltpu.make_async_copy(far, near, load_sem.at[k])
        load.start()
        loads.append(load)

    pending = []

    def send(src, dst, send_sem, recv_sem, other):
        copy = pltpu.make_async_remote_copy(
            src_ref=src, dst_ref=dst, send_sem=send_sem, recv_sem=recv_sem,
            device_id=other, device_id_type=MESH_ID,
        )
        copy.start()
        pending.append(copy)
        return copy

    edges, width = edge_ref.shape
    points = grid_ref.shape[0]
    own = own_ref.shape[0]
    margin = picked.shape[1]
    rows = own + 4 * margin
    send_sel = onehot_rows(send_ref[...], own)
    chosen = t_dot(send_sel, own_ref[...]).astype(BF16)
    for g in range(4):
        picked[g] = chosen[g * margin : (g + 1) * margin]
    pl.semaphore_wait(barrier, len(peers))
    halos = [
        send(picked.at[g], landed.at[slot], hs.at[g], hv.at[slot], other)
        for g, (other, slot) in enumerate(routes)
    ]

    loads[0].wait()
    loads[1].wait()
    proj[rows:, :] = dot(grid_ref[...], w1_ref[2 * width :, :]).astype(BF16)
    grid_t[...] = grid_ref[...].T
    loads[2].wait()

    def prepare(i, carry):
        at = pl.ds(pl.multiple_of(i * edge_block, edge_block), edge_block)
        src = src_ref[at].reshape(1, edge_block)
        dst = dst_ref[at].reshape(1, edge_block)
        sel_t[:rows, at] = onehot_rows(src, rows)
        sel_t[rows:, at] = onehot_rows(dst, points)
        sel[at, :rows] = jnp.concatenate(column_onehot(src, rows), axis=1)
        to_grid = jnp.concatenate(column_onehot(dst, points), axis=1)
        sel[at, rows:] = to_grid
        edge_t[:, at] = edge_ref[at, :].T
        dsw[at, :] = dot(edge_ref[at, :], w1_ref[:width, :]) + dot(to_grid, proj[rows:, :])
        return carry

    lax.fori_loop(0, edges // edge_block, prepare, 0)

    for copy in halos:
        copy.wait_recv()
    table[:own, :] = own_ref[...]
    for g in range(4):
        table[own + g * margin : own + (g + 1) * margin, :] = landed[g]
    proj[:rows, :] = dot(table[...], w1_ref[width : 2 * width, :]).astype(BF16)
    table_t[...] = table[...].T
    loads[3].wait()
    w2_t[...] = w2_ref[...].T

    def forward(i, carry):
        at = pl.ds(pl.multiple_of(i * edge_block, edge_block), edge_block)
        pre = dsw[at, :] + dot(sel[at, :rows], proj[:rows, :])
        sig = sigmoid(pre)
        act = pre * sig
        dsw[at, :] = sig + act * (1.0 - sig)
        normed, scale = layer_stats(dot(act.astype(BF16), w2_ref[...]))
        xhat[at, :] = normed
        rstd[at, :] = jnp.broadcast_to(scale, (edge_block, 128))
        msg[at, :] = (normed * eg_ref[...]).astype(BF16)
        return carry

    lax.fori_loop(0, edges // edge_block, forward, 0)
    for load in loads[4:]:
        load.wait()

    def nodes(i, carry):
        start = pl.multiple_of(i * node_block, node_block)
        at = pl.ds(start, node_block)
        agg = dot(sel_t[pl.ds(rows + start, node_block), :], msg[...]).astype(BF16)
        grid = grid_ref[at, :]
        pre = dot(agg, n1_ref[:width, :]) + dot(grid, n1_ref[width:, :])
        sig = sigmoid(pre)
        normed, scale = layer_stats(dot((pre * sig).astype(BF16), n2_ref[...]))
        out_ref[at, :] = (grid.astype(F32) + normed * ng_ref[...]).astype(BF16)
        cot = cot_ref[at, :].astype(F32)
        draw = layer_back(cot * ng_ref[...], normed, scale)
        dhid = dot_t(draw.astype(BF16), n2_ref[...]).astype(BF16).astype(F32)
        dpre = (dhid * (sig * (1.0 + pre * (1.0 - sig)))).astype(BF16)
        dagg[at, :] = dot_t(dpre, n1_ref[:width, :]).astype(BF16)
        tail[at, :] = cot + dot_t(dpre, n1_ref[width:, :]).astype(BF16).astype(F32)
        return carry

    lax.fori_loop(0, points // node_block, nodes, 0)

    def backward(i, carry):
        at = pl.ds(pl.multiple_of(i * edge_block, edge_block), edge_block)
        dnorm = dot(sel[at, rows:], dagg[...]) * eg_ref[...]
        draw = layer_back(dnorm, xhat[at, :], rstd[at, :1])
        dhid = dot(draw.astype(BF16), w2_t[...]).astype(BF16).astype(F32)
        gp[at, :] = (dhid * dsw[at, :]).astype(BF16)
        return carry

    lax.fori_loop(0, edges // edge_block, backward, 0)

    def put(c, start, value):
        stop = start + value.shape[0]
        for k in range(start // share, -(-stop // share)):
            low, high = max(k * share, start), min((k + 1) * share, stop)
            at = (k // bands // 2, k // bands % 2, k % bands)
            piece = value[low - start : high - start].astype(BF16)
            for j in range(value.shape[1] // wide):
                dw[c + j, at[0], at[1], at[2], low - k * share : high - k * share] = piece[
                    :, j * wide : (j + 1) * wide
                ]

    first, second, third, last = [], [], [], []

    def band_stage(c):
        first[c].wait_recv()
        for o in list(range(1, bands)) + [0]:
            at = band_at[o]
            a0[c, at] = dw[c, :, core, at] + r0[c, :, at]
            if o:
                second.append(
                    send(a0.at[c, at], r1.at[c, o - 1], s1.at[c, o - 1], v1.at[c, o - 1], band_dev[o - 1])
                )

    group = math.gcd(chunks, GROUP)
    for c in range(0, chunks, group):
        low, high = c * wide, (c + group) * wide
        grads = gp[:, low:high]
        part = dot(sel_t[...], grads).astype(BF16)
        red[:, low:high] = part
        put(c, 0, dot(edge_t[...], grads))
        put(c, width, dot(table_t[...], part[:rows]))
        put(c, 2 * width, dot(grid_t[...], part[rows:]))
        for j in range(c, c + group):
            first.append(send(dw.at[j, :, 1 - core], r0.at[j], s0.at[j], v0.at[j], partner))
        for j in range(max(c - group, 0), c):
            band_stage(j)
    grad_table = dot_t(red[:rows, :], w1_ref[width : 2 * width, :])
    for g in range(4):
        gth[g] = grad_table[own + g * margin : own + (g + 1) * margin].astype(BF16)
    backs = [
        send(gth.at[g], ret.at[slot], sh.at[g], vh.at[slot], other)
        for g, (other, slot) in enumerate(routes)
    ]
    for j in range(chunks - group, chunks):
        band_stage(j)
    gg_ref[...] = (tail[...] + dot_t(red[rows:, :], w1_ref[2 * width :, :])).astype(BF16)
    for copy in backs:
        copy.wait_recv()
    returned = ret[...].reshape(4 * margin, width)
    gm_ref[...] = (grad_table[:own] + dot(send_sel, returned)).astype(BF16)

    for c in range(chunks):
        total = a0[c, b].astype(F32)
        for o in range(1, bands):
            second[c * (bands - 1) + o - 1].wait_recv()
            total = total + r1[c, o - 1].astype(F32)
        a1[c] = total.astype(BF16)
        for o in range(1, chips):
            third.append(
                send(a1.at[c, chip_at[o]], r2.at[c, o - 1], s2.at[c, o - 1], v2.at[c, o - 1], chip_dev[o - 1])
            )
    for c in range(chunks):
        total = a1[c, chip].astype(F32)
        for o in range(1, chips):
            third[c * (chips - 1) + o - 1].wait_recv()
            total = total + r2[c, o - 1].astype(F32)
        fin[c] = total.astype(BF16)
        for o in range(1, bands):
            last.append(
                send(fin.at[c], r3.at[c, o - 1], s3.at[c, o - 1], v3.at[c, o - 1], band_dev[o - 1])
            )
        gw_ref[b, :, c * wide : (c + 1) * wide] = fin[c]
    for c in range(chunks):
        for o in range(1, bands):
            last[c * (bands - 1) + o - 1].wait_recv()
            origin = lax.rem(b + bands - o, bands)
            gw_ref[origin, :, c * wide : (c + 1) * wide] = r3[c, o - 1]
    for copy in pending:
        copy.wait_send()


def finish_kernel(grad_scale, out_in, gg_in, gm_in, gw_in, out_ref, gg_ref, gm_ref, gw_ref):
    out_ref[...] = out_in[...]
    gg_ref[...] = gg_in[...]
    gm_ref[...] = gm_in[...]
    gw_ref[...] = gw_in[...].astype(F32) * grad_scale


def decode_step(src, dst, send_row, own, eg, ng, w1, grid, edge, w2, n1, n2, cot):
    edges, width = edge.shape
    points = grid.shape[0]
    margin = send_row.shape[1] // 4
    rows = own.shape[0] + 4 * margin
    bands, sectors = lax.axis_size("band"), lax.axis_size("sector")
    chips = sectors // 2
    share = w1.shape[0] // (bands * sectors)
    chunks = width // math.gcd(width, LANES)
    wide = width // chunks
    dma = pltpu.SemaphoreType.DMA
    whole = (w1, grid, edge, w2, n1, n2, cot)
    results = pl.pallas_call(
        functools.partial(
            step_kernel, edge_block=math.gcd(edges, 768), node_block=math.gcd(points, 512)
        ),
        out_shape=(
            jax.ShapeDtypeStruct((points, width), BF16),
            jax.ShapeDtypeStruct((points, width), BF16),
            jax.ShapeDtypeStruct(own.shape, BF16),
            jax.ShapeDtypeStruct((bands, share, width), BF16),
        ),
        in_specs=[VMEM_SPEC] * 6 + [pl.BlockSpec(memory_space=pl.ANY)] * 7,
        out_specs=(VMEM_SPEC,) * 4,
        scratch_shapes=[pltpu.VMEM(a.shape, a.dtype) for a in whole]
        + [
            dma((len(whole),)),
            pltpu.VMEM((4, margin, width), BF16),
            pltpu.VMEM((4, margin, width), BF16),
            dma((4,)), dma((4,)),
            pltpu.VMEM((rows, width), BF16),
            pltpu.VMEM((rows + points, width), BF16),
            pltpu.VMEM((width, edges), BF16),
            pltpu.VMEM((width, points), BF16),
            pltpu.VMEM((width, rows), BF16),
            pltpu.VMEM((width, width), BF16),
            pltpu.VMEM((rows + points, edges), BF16),
            pltpu.VMEM((edges, rows + points), BF16),
            pltpu.VMEM((edges, width), F32),
            pltpu.VMEM((edges, width), F32),
            pltpu.VMEM((edges, 128), F32),
            pltpu.VMEM((edges, width), BF16),
            pltpu.VMEM((points, width), BF16),
            pltpu.VMEM((points, width), F32),
            pltpu.VMEM((edges, width), BF16),
            pltpu.VMEM((rows + points, width), BF16),
            pltpu.VMEM((chunks, chips, 2, bands, share, wide), BF16),
            pltpu.VMEM((chunks, chips, bands, share, wide), BF16),
            pltpu.VMEM((chunks, bands, chips, share, wide), BF16),
            pltpu.VMEM((chunks, bands - 1, chips, share, wide), BF16),
            pltpu.VMEM((chunks, chips, share, wide), BF16),
            pltpu.VMEM((chunks, chips - 1, share, wide), BF16),
            pltpu.VMEM((chunks, share, wide), BF16),
            pltpu.VMEM((chunks, bands - 1, share, wide), BF16),
            pltpu.VMEM((4, margin, width), BF16),
            pltpu.VMEM((4, margin, width), BF16),
            dma((chunks,)), dma((chunks,)),
            dma((chunks, bands - 1)), dma((chunks, bands - 1)),
            dma((chunks, chips - 1)), dma((chunks, chips - 1)),
            dma((chunks, bands - 1)), dma((chunks, bands - 1)),
            dma((4,)), dma((4,)),
        ],
        compiler_params=pltpu.CompilerParams(
            collective_id=0, has_side_effects=True, vmem_limit_bytes=60 * 1024 * 1024
        ),
    )(src, dst, send_row, own, eg, ng, *whole)
    grad_scale = 1.0 / math.sqrt(edges * bands * sectors)
    return pl.pallas_call(
        functools.partial(finish_kernel, grad_scale),
        out_shape=tuple(
            jax.ShapeDtypeStruct(r.shape, F32 if k == 3 else BF16) for k, r in enumerate(results)
        ),
        in_specs=[VMEM_SPEC] * 4,
        out_specs=(VMEM_SPEC,) * 4,
    )(*results)


def shards(
    grid_lat, mesh_lat, edge_feat, edge_src, edge_dst, send_rows,
    w_edge1, w_edge2, edge_gain, w_node1, w_node2, node_gain, cotangent,
):
    width = w_edge2.shape[0]
    lat_rows, lon_cols = grid_lat.shape[:2]
    points = lat_rows * lon_cols
    out, gg, gm, gw = decode_step(
        edge_src,
        edge_dst,
        send_rows.reshape(1, -1),
        mesh_lat,
        edge_gain.reshape(1, -1),
        node_gain.reshape(1, -1),
        w_edge1,
        grid_lat.reshape(points, width),
        edge_feat,
        w_edge2,
        w_node1,
        w_node2,
        cotangent.reshape(points, width),
    )
    return (
        out.reshape(lat_rows, lon_cols, width),
        gg.reshape(lat_rows, lon_cols, width),
        gm,
        gw.reshape(-1, width),
    )


def solution(mesh):
    in_specs = (
        P("band", "sector", None),
        P(("band", "sector"), None),
        P(("band", "sector"), None),
        P(("band", "sector")),
        P(("band", "sector")),
        P(("band", "sector")),
        P(),
        P(),
        P(),
        P(),
        P(),
        P(),
        P("band", "sector", None),
    )
    out_specs = (
        P("band", "sector", None),
        P("band", "sector", None),
        P(("band", "sector"), None),
        P("sector", None),
    )
    return jax.shard_map(shards, mesh=mesh, in_specs=in_specs, out_specs=out_specs, check_vma=False)
```

```python
import functools
import math

import jax
import jax.numpy as jnp
from jax import lax
from jax.experimental import pallas as pl
from jax.experimental.pallas import tpu as pltpu
from jax.sharding import PartitionSpec as P

EPSILON = 1e-05
MESH_ID = pl.DeviceIdType.MESH
LANES = 128
GROUP = 2
F32 = jnp.float32
BF16 = jnp.bfloat16
VMEM_SPEC = pl.BlockSpec(memory_space=pltpu.VMEM)


def dot(a, b):
    return jnp.dot(a, b, preferred_element_type=F32)


def dot_t(a, b):
    return lax.dot_general(a, b, (((1,), (1,)), ((), ())), preferred_element_type=F32)


def t_dot(a, b):
    return lax.dot_general(a, b, (((0,), (0,)), ((), ())), preferred_element_type=F32)


def onehot_rows(index_row, count):
    width = index_row.shape[1]
    rows = lax.broadcasted_iota(jnp.int16, (count, width), 0)
    hit = rows == jnp.broadcast_to(index_row.astype(jnp.int16), (count, width))
    return jnp.where(hit, jnp.ones((), BF16), jnp.zeros((), BF16))


def neighbours():
    sectors, bands = lax.axis_size("sector"), lax.axis_size("band")
    s, b = lax.axis_index("sector"), lax.axis_index("band")
    below = {"sector": lax.rem(s + sectors - 1, sectors)}
    above = {"sector": lax.rem(s + 1, sectors)}
    band_below = {"band": lax.rem(b + bands - 1, bands)}
    band_above = {"band": lax.rem(b + 1, bands)}
    return below, above, band_below, band_above


def sigmoid(v):
    return 0.5 * jnp.tanh(0.5 * v) + 0.5


def layer_stats(raw):
    centred = raw - jnp.mean(raw, axis=-1, keepdims=True)
    scale = lax.rsqrt(jnp.mean(centred * centred, axis=-1, keepdims=True) + EPSILON)
    return centred * scale, scale


def layer_back(dnorm, normed, scale):
    return scale * (
        dnorm
        - jnp.mean(dnorm, axis=-1, keepdims=True)
        - normed * jnp.mean(dnorm * normed, axis=-1, keepdims=True)
    )


def column_onehot(index_row, count):
    columns = jnp.broadcast_to(index_row, (128, index_row.shape[1])).T
    columns = columns.astype(jnp.int16)
    lanes = lax.broadcasted_iota(jnp.int16, columns.shape, 1)
    one, zero = jnp.ones((), BF16), jnp.zeros((), BF16)
    return [
        jnp.where(columns - jnp.int16(k) == lanes, one, zero) for k in range(0, count, 128)
    ]


def step_kernel(
    src_ref, dst_ref, send_ref, own_ref, eg_ref, ng_ref,
    w1_hbm, grid_hbm, edge_hbm, w2_hbm, n1_hbm, n2_hbm, cot_hbm,
    out_ref, gg_ref, gm_ref, gw_ref,
    w1_ref, grid_ref, edge_ref, w2_ref, n1_ref, n2_ref, cot_ref, load_sem,
    picked, landed, hs, hv,
    table, proj, edge_t, grid_t, table_t, w2_t, sel_t, sel, dsw, xhat, rstd, msg, dagg, tail, gp, red,
    dw, r0, a0, r1, a1, r2, fin, r3, gth, ret,
    s0, v0, s1, v1, s2, v2, s3, v3, sh, vh,
    *, edge_block, node_block,
):
    chunks, chips, bands, share, wide = r0.shape
    sectors = 2 * chips
    s, b = lax.axis_index("sector"), lax.axis_index("band")
    core, chip = lax.rem(s, 2), lax.div(s, 2)
    partner = {"sector": s + 1 - 2 * core}
    other_side = {"sector": lax.rem(s + 2 * core - 1 + sectors, sectors)}
    below, above, band_below, band_above = neighbours()
    band_at = [lax.rem(b + o, bands) for o in range(bands)]
    chip_at = [lax.rem(chip + o, chips) for o in range(chips)]
    band_dev = [{"band": band_at[o]} for o in range(1, bands)]
    chip_dev = [{"sector": 2 * chip_at[o] + core} for o in range(1, chips)]
    routes = ((below, 1), (above, 0), (band_below, 3), (band_above, 2))

    barrier = pltpu.get_barrier_semaphore()
    peers = [partner, other_side] + band_dev + chip_dev
    for other in peers:
        pl.semaphore_signal(barrier, inc=1, device_id=other, device_id_type=MESH_ID)

    loads = []
    pairs = (
        (w1_hbm, w1_ref), (grid_hbm, grid_ref), (edge_hbm, edge_ref), (w2_hbm, w2_ref),
        (n1_hbm, n1_ref), (n2_hbm, n2_ref), (cot_hbm, cot_ref),
    )
    for k, (far, near) in enumerate(pairs):
        load = pltpu.make_async_copy(far, near, load_sem.at[k])
        load.start()
        loads.append(load)

    pending = []

    def send(src, dst, send_sem, recv_sem, other):
        copy = pltpu.make_async_remote_copy(
            src_ref=src, dst_ref=dst, send_sem=send_sem, recv_sem=recv_sem,
            device_id=other, device_id_type=MESH_ID,
        )
        copy.start()
        pending.append(copy)
        return copy

    edges, width = edge_ref.shape
    points = grid_ref.shape[0]
    own = own_ref.shape[0]
    margin = picked.shape[1]
    rows = own + 4 * margin
    send_sel = onehot_rows(send_ref[...], own)
    chosen = t_dot(send_sel, own_ref[...]).astype(BF16)
    for g in range(4):
        picked[g] = chosen[g * margin : (g + 1) * margin]
    pl.semaphore_wait(barrier, len(peers))
    halos = [
        send(picked.at[g], landed.at[slot], hs.at[g], hv.at[slot], other)
        for g, (other, slot) in enumerate(routes)
    ]

    loads[0].wait()
    loads[1].wait()
    proj[rows:, :] = dot(grid_ref[...], w1_ref[2 * width :, :]).astype(BF16)
    grid_t[...] = grid_ref[...].T
    loads[2].wait()

    def prepare(i, carry):
        at = pl.ds(pl.multiple_of(i * edge_block, edge_block), edge_block)
        src = src_ref[at].reshape(1, edge_block)
        dst = dst_ref[at].reshape(1, edge_block)
        sel_t[:rows, at] = onehot_rows(src, rows)
        sel_t[rows:, at] = onehot_rows(dst, points)
        sel[at, :rows] = jnp.concatenate(column_onehot(src, rows), axis=1)
        to_grid = jnp.concatenate(column_onehot(dst, points), axis=1)
        sel[at, rows:] = to_grid
        edge_t[:, at] = edge_ref[at, :].T
        dsw[at, :] = dot(edge_ref[at, :], w1_ref[:width, :]) + dot(to_grid, proj[rows:, :])
        return carry

    lax.fori_loop(0, edges // edge_block, prepare, 0)

    loads[3].wait()
    w2_t[...] = w2_ref[...].T
    for copy in halos:
        copy.wait_recv()
    table[:own, :] = own_ref[...]
    for g in range(4):
        table[own + g * margin : own + (g + 1) * margin, :] = landed[g]
    proj[:rows, :] = dot(table[...], w1_ref[width : 2 * width, :]).astype(BF16)
    table_t[...] = table[...].T

    def forward(i, carry):
        at = pl.ds(pl.multiple_of(i * edge_block, edge_block), edge_block)
        pre = dsw[at, :] + dot(sel[at, :rows], proj[:rows, :])
        sig = sigmoid(pre)
        act = pre * sig
        dsw[at, :] = sig + act * (1.0 - sig)
        normed, scale = layer_stats(dot(act.astype(BF16), w2_ref[...]))
        xhat[at, :] = normed
        rstd[at, :] = jnp.broadcast_to(scale, (edge_block, 128))
        msg[at, :] = (normed * eg_ref[...]).astype(BF16)
        return carry

    lax.fori_loop(0, edges // edge_block, forward, 0)
    for load in loads[4:]:
        load.wait()

    def nodes(i, carry):
        start = pl.multiple_of(i * node_block, node_block)
        at = pl.ds(start, node_block)
        agg = dot(sel_t[pl.ds(rows + start, node_block), :], msg[...]).astype(BF16)
        grid = grid_ref[at, :]
        pre = dot(agg, n1_ref[:width, :]) + dot(grid, n1_ref[width:, :])
        sig = sigmoid(pre)
        normed, scale = layer_stats(dot((pre * sig).astype(BF16), n2_ref[...]))
        out_ref[at, :] = (grid.astype(F32) + normed * ng_ref[...]).astype(BF16)
        cot = cot_ref[at, :].astype(F32)
        draw = layer_back(cot * ng_ref[...], normed, scale)
        dhid = dot_t(draw.astype(BF16), n2_ref[...]).astype(BF16).astype(F32)
        dpre = (dhid * (sig * (1.0 + pre * (1.0 - sig)))).astype(BF16)
        dagg[at, :] = dot_t(dpre, n1_ref[:width, :]).astype(BF16)
        tail[at, :] = cot + dot_t(dpre, n1_ref[width:, :]).astype(BF16).astype(F32)
        return carry

    lax.fori_loop(0, points // node_block, nodes, 0)

    def backward(i, carry):
        at = pl.ds(pl.multiple_of(i * edge_block, edge_block), edge_block)
        dnorm = dot(sel[at, rows:], dagg[...]) * eg_ref[...]
        draw = layer_back(dnorm, xhat[at, :], rstd[at, :1])
        msg[at, :] = draw.astype(BF16)
        return carry

    lax.fori_loop(0, edges // edge_block, backward, 0)

    def put(c, start, value):
        stop = start + value.shape[0]
        for k in range(start // share, -(-stop // share)):
            low, high = max(k * share, start), min((k + 1) * share, stop)
            at = (k // bands // 2, k // bands % 2, k % bands)
            piece = value[low - start : high - start].astype(BF16)
            for j in range(value.shape[1] // wide):
                dw[c + j, at[0], at[1], at[2], low - k * share : high - k * share] = piece[
                    :, j * wide : (j + 1) * wide
                ]

    first, second, third, last = [], [], [], []

    def band_stage(c):
        first[c].wait_recv()
        for o in list(range(1, bands)) + [0]:
            at = band_at[o]
            a0[c, at] = dw[c, :, core, at] + r0[c, :, at]
            if o:
                second.append(
                    send(a0.at[c, at], r1.at[c, o - 1], s1.at[c, o - 1], v1.at[c, o - 1], band_dev[o - 1])
                )

    group = math.gcd(chunks, GROUP)
    for c in range(0, chunks, group):
        low, high = c * wide, (c + group) * wide

        def columns(i, carry):
            at = pl.ds(pl.multiple_of(i * edge_block, edge_block), edge_block)
            dhid = dot(msg[at, :], w2_t[:, low:high]).astype(BF16).astype(F32)
            gp[at, low:high] = (dhid * dsw[at, low:high]).astype(BF16)
            return carry

        lax.fori_loop(0, edges // edge_block, columns, 0)
        grads = gp[:, low:high]
        part = dot(sel_t[...], grads).astype(BF16)
        red[:, low:high] = part
        for j in range(max(c - group, 0), c):
            band_stage(j)
        put(c, 0, dot(edge_t[...], grads))
        put(c, width, dot(table_t[...], part[:rows]))
        put(c, 2 * width, dot(grid_t[...], part[rows:]))
        for j in range(c, c + group):
            first.append(send(dw.at[j, :, 1 - core], r0.at[j], s0.at[j], v0.at[j], partner))
    grad_table = dot_t(red[:rows, :], w1_ref[width : 2 * width, :])
    for g in range(4):
        gth[g] = grad_table[own + g * margin : own + (g + 1) * margin].astype(BF16)
    backs = [
        send(gth.at[g], ret.at[slot], sh.at[g], vh.at[slot], other)
        for g, (other, slot) in enumerate(routes)
    ]
    for j in range(chunks - group, chunks):
        band_stage(j)
    gg_ref[...] = (tail[...] + dot_t(red[rows:, :], w1_ref[2 * width :, :])).astype(BF16)
    for copy in backs:
        copy.wait_recv()
    returned = ret[...].reshape(4 * margin, width)
    gm_ref[...] = (grad_table[:own] + dot(send_sel, returned)).astype(BF16)

    for c in range(chunks):
        total = a0[c, b].astype(F32)
        for o in range(1, bands):
            second[c * (bands - 1) + o - 1].wait_recv()
            total = total + r1[c, o - 1].astype(F32)
        a1[c] = total.astype(BF16)
        for o in range(1, chips):
            third.append(
                send(a1.at[c, chip_at[o]], r2.at[c, o - 1], s2.at[c, o - 1], v2.at[c, o - 1], chip_dev[o - 1])
            )
    for c in range(chunks):
        total = a1[c, chip].astype(F32)
        for o in range(1, chips):
            third[c * (chips - 1) + o - 1].wait_recv()
            total = total + r2[c, o - 1].astype(F32)
        fin[c] = total.astype(BF16)
        for o in range(1, bands):
            last.append(
                send(fin.at[c], r3.at[c, o - 1], s3.at[c, o - 1], v3.at[c, o - 1], band_dev[o - 1])
            )
        gw_ref[b, :, c * wide : (c + 1) * wide] = fin[c]
    for c in range(chunks):
        for o in range(1, bands):
            last[c * (bands - 1) + o - 1].wait_recv()
            origin = lax.rem(b + bands - o, bands)
            gw_ref[origin, :, c * wide : (c + 1) * wide] = r3[c, o - 1]
    for copy in pending:
        copy.wait_send()


def finish_kernel(grad_scale, out_in, gg_in, gm_in, gw_in, out_ref, gg_ref, gm_ref, gw_ref):
    out_ref[...] = out_in[...]
    gg_ref[...] = gg_in[...]
    gm_ref[...] = gm_in[...]
    gw_ref[...] = gw_in[...].astype(F32) * grad_scale


def decode_step(src, dst, send_row, own, eg, ng, w1, grid, edge, w2, n1, n2, cot):
    edges, width = edge.shape
    points = grid.shape[0]
    margin = send_row.shape[1] // 4
    rows = own.shape[0] + 4 * margin
    bands, sectors = lax.axis_size("band"), lax.axis_size("sector")
    chips = sectors // 2
    share = w1.shape[0] // (bands * sectors)
    chunks = width // math.gcd(width, LANES)
    wide = width // chunks
    dma = pltpu.SemaphoreType.DMA
    whole = (w1, grid, edge, w2, n1, n2, cot)
    results = pl.pallas_call(
        functools.partial(
            step_kernel, edge_block=math.gcd(edges, 768), node_block=math.gcd(points, 512)
        ),
        out_shape=(
            jax.ShapeDtypeStruct((points, width), BF16),
            jax.ShapeDtypeStruct((points, width), BF16),
            jax.ShapeDtypeStruct(own.shape, BF16),
            jax.ShapeDtypeStruct((bands, share, width), BF16),
        ),
        in_specs=[VMEM_SPEC] * 6 + [pl.BlockSpec(memory_space=pl.ANY)] * 7,
        out_specs=(VMEM_SPEC,) * 4,
        scratch_shapes=[pltpu.VMEM(a.shape, a.dtype) for a in whole]
        + [
            dma((len(whole),)),
            pltpu.VMEM((4, margin, width), BF16),
            pltpu.VMEM((4, margin, width), BF16),
            dma((4,)), dma((4,)),
            pltpu.VMEM((rows, width), BF16),
            pltpu.VMEM((rows + points, width), BF16),
            pltpu.VMEM((width, edges), BF16),
            pltpu.VMEM((width, points), BF16),
            pltpu.VMEM((width, rows), BF16),
            pltpu.VMEM((width, width), BF16),
            pltpu.VMEM((rows + points, edges), BF16),
            pltpu.VMEM((edges, rows + points), BF16),
            pltpu.VMEM((edges, width), F32),
            pltpu.VMEM((edges, width), F32),
            pltpu.VMEM((edges, 128), F32),
            pltpu.VMEM((edges, width), BF16),
            pltpu.VMEM((points, width), BF16),
            pltpu.VMEM((points, width), F32),
            pltpu.VMEM((edges, width), BF16),
            pltpu.VMEM((rows + points, width), BF16),
            pltpu.VMEM((chunks, chips, 2, bands, share, wide), BF16),
            pltpu.VMEM((chunks, chips, bands, share, wide), BF16),
            pltpu.VMEM((chunks, bands, chips, share, wide), BF16),
            pltpu.VMEM((chunks, bands - 1, chips, share, wide), BF16),
            pltpu.VMEM((chunks, chips, share, wide), BF16),
            pltpu.VMEM((chunks, chips - 1, share, wide), BF16),
            pltpu.VMEM((chunks, share, wide), BF16),
            pltpu.VMEM((chunks, bands - 1, share, wide), BF16),
            pltpu.VMEM((4, margin, width), BF16),
            pltpu.VMEM((4, margin, width), BF16),
            dma((chunks,)), dma((chunks,)),
            dma((chunks, bands - 1)), dma((chunks, bands - 1)),
            dma((chunks, chips - 1)), dma((chunks, chips - 1)),
            dma((chunks, bands - 1)), dma((chunks, bands - 1)),
            dma((4,)), dma((4,)),
        ],
        compiler_params=pltpu.CompilerParams(
            collective_id=0, has_side_effects=True, vmem_limit_bytes=60 * 1024 * 1024
        ),
    )(src, dst, send_row, own, eg, ng, *whole)
    grad_scale = 1.0 / math.sqrt(edges * bands * sectors)
    return pl.pallas_call(
        functools.partial(finish_kernel, grad_scale),
        out_shape=tuple(
            jax.ShapeDtypeStruct(r.shape, F32 if k == 3 else BF16) for k, r in enumerate(results)
        ),
        in_specs=[VMEM_SPEC] * 4,
        out_specs=(VMEM_SPEC,) * 4,
    )(*results)


def shards(
    grid_lat, mesh_lat, edge_feat, edge_src, edge_dst, send_rows,
    w_edge1, w_edge2, edge_gain, w_node1, w_node2, node_gain, cotangent,
):
    width = w_edge2.shape[0]
    lat_rows, lon_cols = grid_lat.shape[:2]
    points = lat_rows * lon_cols
    out, gg, gm, gw = decode_step(
        edge_src,
        edge_dst,
        send_rows.reshape(1, -1),
        mesh_lat,
        edge_gain.reshape(1, -1),
        node_gain.reshape(1, -1),
        w_edge1,
        grid_lat.reshape(points, width),
        edge_feat,
        w_edge2,
        w_node1,
        w_node2,
        cotangent.reshape(points, width),
    )
    return (
        out.reshape(lat_rows, lon_cols, width),
        gg.reshape(lat_rows, lon_cols, width),
        gm,
        gw.reshape(-1, width),
    )


def solution(mesh):
    in_specs = (
        P("band", "sector", None),
        P(("band", "sector"), None),
        P(("band", "sector"), None),
        P(("band", "sector")),
        P(("band", "sector")),
        P(("band", "sector")),
        P(),
        P(),
        P(),
        P(),
        P(),
        P(),
        P("band", "sector", None),
    )
    out_specs = (
        P("band", "sector", None),
        P("band", "sector", None),
        P(("band", "sector"), None),
        P("sector", None),
    )
    return jax.shard_map(shards, mesh=mesh, in_specs=in_specs, out_specs=out_specs, check_vma=False)
```
